32 devices in a mesh: grp: 2 (over y), mom: 16 (over z, x, core).
Axes of the slice: x: 2, y: 2, z: 4, core: 2. Of those that a mesh axis runs over, the one named last changes fastest.
Arguments:
- green_function: bfloat16 [2, 4096, 512], P(None, ('grp', 'mom')), parts along dimension 1, may hold values from -0.8984375 to 0.8984375
- couplings: bfloat16 [8, 2, 512, 512], replicated, may hold values from -0.1875 to 0.1875
- phonon_modes: int32 [3, 4], replicated, may hold values from 0 to 7
- weights: float32 [3, 4], replicated, may hold values from 0.5 to 2
Outputs:
- self_energy: float32 [2, 4096, 512], P(None, ('grp', 'mom')), parts along dimension 1
The draws below stay inside these ranges and needn't reach their ends.
There are 2 independent parts, one for each index of `grp`. The reference program is written for one: setup_inputs(seed, part) draws one part's arguments, and reference() takes and returns one part's arrays. A program takes and returns all parts, laid end to end along the dimension named above; an argument that names none is the same for every part. Nothing has to cross between parts.
Inputs may be any that keep to these rules, and one draw needn't show every extreme that they name: `phonon_modes`: each entry names one matrix of couplings.
All inputs are finite; a program needn't handle non-finite values.
Results may differ from the reference program's by a relative error of at most 0.0042.
Values may be sent and summed in bfloat16 or wider, within the bound.
No kernel may reach another device: no remote copies, remote signals or barrier semaphores. Data moves between devices by JAX's collectives and lax.ppermute only.
A program may use at most 64 MiB of HBM per device.

```python
import math
import jax
import jax.numpy as jnp
from jax import lax

SLAB = 512
NK = 4
ROWS = 2048
HALF = 1
STOPS = 3
MODES = 4
BANK = 8


def set_ends(drawn, own_key, smallest, high):
    longest = drawn.shape.index(max(drawn.shape))
    spots = []
    for shift in (0, 1):
        where = [jax.random.randint(jax.random.fold_in(own_key, axis), (), 0, length) for axis, length in enumerate(drawn.shape)]
        where[longest] = (where[longest] + shift) % drawn.shape[longest]
        spots.append(tuple(where))
    return drawn.at[spots[0]].set(smallest).at[spots[1]].set(high)


def block_scale(own_key, dims, pieces, smallest, largest):
    gain = 1.0
    for position, parts in pieces:
        draws = jax.random.uniform(jax.random.fold_in(jax.random.fold_in(own_key, 6), position), (parts,), jnp.float32, smallest / len(pieces), largest / len(pieces))
        gain = gain * jnp.repeat(jnp.exp(draws), dims[position] // parts).reshape((-1,) + (1,) * (len(dims) - 1 - position))
    return gain


def normal_values(key, shape, deviation, most, shards=(), kind=jnp.bfloat16):
    values = deviation * jax.random.normal(key, shape, jnp.float32)
    if shards:
        values = values * block_scale(key, shape, shards, -0.22, 0.18)
    return jnp.clip(values, -most, most).astype(kind)


def setup_inputs(seed: int = 0, part: int = 0) -> dict:
    seeds = jax.random.split(jax.random.key(seed), 5)
    part_keys = jax.random.split(jax.random.fold_in(seeds[4], part), 5)
    return {
        "green_function": normal_values(part_keys[0], (2, ROWS, SLAB), 0.15, 0.8984375, ((1, 16),)),
        "couplings": normal_values(seeds[1], (BANK, 2, SLAB, SLAB), (2 * SLAB) ** -0.5, 0.1875),
        "phonon_modes": set_ends(jax.random.randint(seeds[2], (STOPS, MODES), 0, BANK), jax.random.fold_in(seeds[2], 1), 0, BANK - 1).astype(jnp.int32),
        "weights": jnp.clip(jnp.exp(jax.random.uniform(seeds[3], (STOPS, MODES), jnp.float32, math.log(0.5), math.log(2.0))), 0.5, 2.0),
    }


def spectral_of(green_block):
    real_part = green_block[0].astype(jnp.float32)
    imag_part = green_block[1].astype(jnp.float32)
    spec_real = -(imag_part + imag_part.T)
    spec_imag = real_part - real_part.T
    return jnp.stack([spec_real, spec_imag]).astype(jnp.bfloat16)


def stack_spectral(spectral):
    upper_half = jnp.concatenate([spectral[0], spectral[1]], axis=1)
    lower_half = jnp.concatenate([-spectral[1], spectral[0]], axis=1)
    return jnp.concatenate([upper_half, lower_half], axis=0)


def stack_coupling(coupling):
    upper_half = jnp.concatenate([coupling[0], coupling[1]], axis=1)
    lower_half = jnp.concatenate([-coupling[1], coupling[0]], axis=1)
    return jnp.concatenate([upper_half, lower_half], axis=0)


def reference(green_function, couplings, phonon_modes, weights):
    blocks = green_function.reshape(2, NK, SLAB, SLAB).transpose(1, 0, 2, 3)
    spectra = lax.map(spectral_of, blocks)

    def one_momentum(momentum):
        accumulated = jnp.zeros((SLAB, 2 * SLAB), jnp.float32)
        for stop_index in range(STOPS):
            source = (momentum + HALF - stop_index) % NK
            spectral = lax.dynamic_index_in_dim(spectra, source.astype(jnp.int32), 0, keepdims=False)
            stacked = stack_spectral(spectral)
            for mode_index in range(MODES):
                coupling = lax.dynamic_index_in_dim(couplings, phonon_modes[stop_index, mode_index], 0, keepdims=False)
                left_rows = jnp.concatenate([coupling[0], coupling[1]], axis=1)
                product = jnp.dot(left_rows, stacked, preferred_element_type=jnp.float32).astype(jnp.bfloat16)
                right_side = stack_coupling(coupling)
                contribution = lax.dot_general(product, right_side, (((1,), (1,)), ((), ())), preferred_element_type=jnp.float32)
                accumulated = accumulated + weights[stop_index, mode_index] * contribution
        return accumulated

    self_energy = lax.map(one_momentum, jnp.arange(NK, dtype=jnp.int32))
    return self_energy.reshape(NK, SLAB, 2, SLAB).transpose(2, 0, 1, 3).reshape(2, NK * SLAB, SLAB)
```

```python
import functools

import jax
import jax.numpy as jnp
from jax import lax
from jax.experimental import pallas as pl
from jax.experimental.pallas import tpu as pltpu
from jax.sharding import PartitionSpec as P

F32 = jnp.float32
BF16 = jnp.bfloat16


def partner(block, axis, bit):
    count = lax.axis_size(axis)
    route = [(i, i ^ 1 << bit) for i in range(count)]
    return lax.ppermute(block, axis, route)


def passed_along(block, axis, distance):
    count = lax.axis_size(axis)
    route = [((i - distance) % count, i) for i in range(count)]
    return lax.ppermute(block, axis, route)


def gathered(block, axis, levels):
    have = {0: block}
    for level in reversed(range(levels)):
        for offset in list(have):
            have[offset | 1 << level] = partner(have[offset], axis, level)
    return [have[offset] for offset in sorted(have)]


def adjoint_rows_kernel(modes, member, *refs):
    *rows, out = refs
    for mode, row in enumerate(rows):
        tile = row.shape[2]
        out[0, mode, :, :tile] = row[0, 0].T
        out[0, mode, :, tile:] = row[0, 1].T


def adjoint_rows(couplings, phonon_modes, member, tile):
    stops, modes = phonon_modes.shape
    slab = couplings.shape[3]

    def spec(mode):
        return pl.BlockSpec((1, 2, tile, slab), lambda s, table, me: (table[s, mode], 0, me[0], 0))

    return pl.pallas_call(
        adjoint_rows_kernel,
        grid_spec=pltpu.PrefetchScalarGridSpec(
            num_scalar_prefetch=2,
            grid=(stops,),
            in_specs=[spec(mode) for mode in range(modes)],
            out_specs=pl.BlockSpec((1, modes, slab, 2 * tile), lambda s, table, me: (s, 0, 0, 0)),
        ),
        out_shape=jax.ShapeDtypeStruct((stops, modes, slab, 2 * tile), BF16),
        compiler_params=pltpu.CompilerParams(vmem_limit_bytes=16 << 20),
        cost_estimate=pl.CostEstimate(flops=0, transcendentals=0, bytes_accessed=6 << 20),
        name="adjoint_rows",
    )(phonon_modes, member, *[couplings] * modes)


def fill_spectral(me, blocks, green, spectral):
    tile, slab = blocks[0].shape[1:]
    for offset, block in enumerate(blocks):
        row = pl.multiple_of((me ^ offset) * tile, tile)
        green[:, pl.ds(row, tile), :] = block[...]
    spots = [slice(i * tile, (i + 1) * tile) for i in range(slab // tile)]
    for i, rows in enumerate(spots):
        for j, cols in enumerate(spots):
            here = slice(slab + j * tile, slab + (j + 1) * tile)
            real = -(green[1, rows, cols].astype(F32) + green[1, cols, rows].T.astype(F32))
            imag = green[0, rows, cols].astype(F32) - green[0, cols, rows].T.astype(F32)
            spectral[rows, cols] = real.astype(BF16)
            spectral[rows, here] = imag.astype(BF16)


def add_modes(stop, modes, weights, spectral, adjoint, couplings, held, sems, total):
    count = adjoint.shape[0]
    half = adjoint.shape[2] // 2
    for mode in range(count):
        turned = adjoint[mode]
        real, imag = turned[:, :half], turned[:, half:]
        right = jnp.concatenate(
            [jnp.concatenate([real, -imag], axis=1), turned_swap(imag, real)], axis=0
        )
        product = jnp.dot(spectral[...], right, preferred_element_type=F32).astype(BF16)
        real, imag = product[:, :half], product[:, half:]
        right = jnp.concatenate([product, turned_swap(-imag, real)], axis=0)
        coupling_copy(stop, mode, modes, couplings, held, sems).wait()
        left = jnp.concatenate([held[mode, 0], held[mode, 1]], axis=1)
        term = weights[stop, mode] * jnp.dot(left, right, preferred_element_type=F32)
        if total is None:
            total = term
        else:
            total = total + term
    return total


def turned_swap(first, second):
    return jnp.concatenate([first, second], axis=1)


def coupling_copy(stop, mode, modes, couplings, held, sems):
    return pltpu.make_async_copy(couplings.at[modes[stop, mode]], held.at[mode], sems.at[mode])


def start_copies(stop, count, modes, couplings, held, sems):
    for mode in range(count):
        coupling_copy(stop, mode, modes, couplings, held, sems).start()


def later_kernel(stop, count, modes, weights, member, *refs):
    blocks = refs[:count]
    adjoint, couplings, term, spectral, green, held, sems = refs[count:]
    start_copies(stop, adjoint.shape[0], modes, couplings, held, sems)
    fill_spectral(member[0], blocks, green, spectral)
    total = add_modes(stop, modes, weights, spectral, adjoint, couplings, held, sems, None)
    term[...] = total.astype(BF16)


def own_kernel(stop, modes, weights, spectral, adjoint, couplings, term, held, sems):
    start_copies(stop, adjoint.shape[0], modes, couplings, held, sems)
    term[...] = add_modes(stop, modes, weights, spectral, adjoint, couplings, held, sems, None)


def last_kernel(stop, count, modes, weights, member, *refs):
    blocks = refs[:count]
    adjoint, couplings, own, arrived, out, spectral, green, held, sems = refs[count:]
    start_copies(stop, adjoint.shape[0], modes, couplings, held, sems)
    fill_spectral(member[0], blocks, green, spectral)
    total = own[...] + arrived[...].astype(F32)
    total = add_modes(stop, modes, weights, spectral, adjoint, couplings, held, sems, total)
    tile = out.shape[1]
    out[0] = total[:, :tile].T
    out[1] = -total[:, tile:].T


def body(green_function, couplings, phonon_modes, weights):
    tile, slab = green_function.shape[1:]
    group = slab // tile
    levels = group.bit_length() - 1
    modes = phonon_modes.shape[1]
    member = (lax.axis_index("mom") % group).astype(jnp.int32).reshape(1)

    smem = pl.BlockSpec(memory_space=pltpu.SMEM)
    vmem = pl.BlockSpec(memory_space=pltpu.VMEM)
    anywhere = pl.BlockSpec(memory_space=pl.ANY)
    columns = (slab, 2 * tile)
    held = [pltpu.VMEM((modes, 2, slab, slab), BF16), pltpu.SemaphoreType.DMA((modes,))]
    green = pltpu.VMEM((2, slab, slab), BF16)
    params = pltpu.CompilerParams(vmem_limit_bytes=24 << 20)
    cost = pl.CostEstimate(
        flops=modes * 2 * 2 * slab * 2 * slab * 2 * tile,
        transcendentals=0,
        bytes_accessed=(modes + 2) * 2 * slab * slab * 2,
    )

    incoming = passed_along(green_function, "mom", group)
    own_blocks = gathered(green_function, "mom", levels)
    adjoint = adjoint_rows(couplings, phonon_modes, member, tile)
    next_blocks = gathered(incoming, "mom", levels)

    leaving, spectral = pl.pallas_call(
        functools.partial(later_kernel, 0, group),
        in_specs=[smem] * 3 + [vmem] * (group + 1) + [anywhere],
        out_specs=[vmem, vmem],
        out_shape=[
            jax.ShapeDtypeStruct(columns, BF16),
            jax.ShapeDtypeStruct((slab, 2 * slab), BF16),
        ],
        scratch_shapes=[green, *held],
        compiler_params=params,
        cost_estimate=cost,
        name="later_stop",
    )(phonon_modes, weights, member, *own_blocks, adjoint[0], couplings)
    arrived = passed_along(leaving, "mom", -group)

    own = pl.pallas_call(
        functools.partial(own_kernel, 1),
        in_specs=[smem] * 2 + [vmem] * 2 + [anywhere],
        out_specs=vmem,
        out_shape=jax.ShapeDtypeStruct(columns, F32),
        scratch_shapes=held,
        compiler_params=params,
        cost_estimate=cost,
        name="own_stop",
    )(phonon_modes, weights, spectral, adjoint[1], couplings)

    return pl.pallas_call(
        functools.partial(last_kernel, 2, group),
        in_specs=[smem] * 3 + [vmem] * (group + 1) + [anywhere] + [vmem] * 2,
        out_specs=vmem,
        out_shape=jax.ShapeDtypeStruct((2, tile, slab), F32),
        scratch_shapes=[pltpu.VMEM((slab, 2 * slab), BF16), green, *held],
        compiler_params=params,
        cost_estimate=cost,
        name="last_stop",
    )(phonon_modes, weights, member, *next_blocks, adjoint[2], couplings, own, arrived)


def solution(mesh):
    in_specs = (P(None, ("grp", "mom"), None), P(), P(), P())
    out_specs = P(None, ("grp", "mom"), None)
    return jax.shard_map(body, mesh=mesh, in_specs=in_specs, out_specs=out_specs, check_vma=False)
```

```python
import jax
import jax.numpy as jnp
from jax import lax
from jax.experimental import pallas as pl
from jax.experimental.pallas import tpu as pltpu
from jax.sharding import PartitionSpec as P

F32 = jnp.float32
BF16 = jnp.bfloat16
VMEM = pl.BlockSpec(memory_space=pltpu.VMEM)
HBM = pl.BlockSpec(memory_space=pltpu.HBM)


def partner(block, axis, bit):
    count = lax.axis_size(axis)
    return lax.ppermute(block, axis, [(i, i ^ 1 << bit) for i in range(count)])


def passed_along(block, axis, distance):
    count = lax.axis_size(axis)
    return lax.ppermute(block, axis, [((i - distance) % count, i) for i in range(count)])


def gathered(block, axis, levels, before):
    have = {0: block}
    for level in reversed(range(levels)):
        for offset in list(have):
            moving = have[offset] if offset == 0 else after(have[offset], before)
            have[offset | 1 << level] = partner(moving, axis, level)
    return [have[offset] for offset in sorted(have)]


def after(value, before):
    return lax.optimization_barrier((value, before))[0]


def beside(first, second):
    return jnp.concatenate([first, second], axis=1)


def own_row(offset, group, tile):
    member = lax.axis_index("mom") % group
    return pl.multiple_of((member ^ offset) * tile, tile)


def prepare_kernel(listed, couplings, *refs):
    *outs, modes, listed_sem, sems = refs
    listing = pltpu.make_async_copy(listed, modes, listed_sem)
    listing.start()
    listing.wait()
    picked, turned = outs[::2], outs[1::2]
    stops, count = modes.shape
    slab = couplings.shape[3]
    tile = turned[0].shape[2] // 2
    copies = [
        [
            pltpu.make_async_copy(couplings.at[modes[stop, mode]], picked[stop].at[mode], sems.at[stop, mode])
            for mode in range(count)
        ]
        for stop in range(stops)
    ]
    for row in copies:
        for copy in row:
            copy.start()
    rows = pl.ds(own_row(0, slab // tile, tile), tile)
    for stop in range(stops):
        for mode in range(count):
            copies[stop][mode].wait()
            turned[stop][mode, :, :tile] = picked[stop][mode, 0, rows, :].T
            turned[stop][mode, :, tile:] = picked[stop][mode, 1, rows, :].T


def fill_spectral(blocks, spectral):
    tile, slab = blocks[0].shape[1:]
    starts = [own_row(offset, len(blocks), tile) for offset in range(len(blocks))]
    spots = [pl.ds(start, tile) for start in starts]
    imag_spots = [pl.ds(slab + start, tile) for start in starts]
    for i, block in enumerate(blocks):
        for j, other in enumerate(blocks):
            real = -(block[1, :, spots[j]].astype(F32) + other[1, :, spots[i]].T.astype(F32))
            imag = block[0, :, spots[j]].astype(F32) - other[0, :, spots[i]].T.astype(F32)
            spectral[spots[i], spots[j]] = real.astype(BF16)
            spectral[spots[i], imag_spots[j]] = imag.astype(BF16)


def stop_term(stop, weights, spectral, turned, picked, start):
    count, slab, width = turned.shape
    tile = width // 2
    rights = []
    for mode in range(count):
        real, imag = turned[mode, :, :tile], turned[mode, :, tile:]
        rights.append(jnp.concatenate([beside(real, -imag), beside(imag, real)], axis=0))
    products = jnp.dot(
        spectral[...], jnp.concatenate(rights, axis=1), preferred_element_type=F32
    ).astype(BF16)
    total = start
    for mode in range(count):
        product = products[:, mode * width : (mode + 1) * width]
        real, imag = product[:, :tile], product[:, tile:]
        right = jnp.concatenate([product, beside(-imag, real)], axis=0)
        left = beside(picked[mode, 0], picked[mode, 1])
        term = weights[stop : stop + 1, mode : mode + 1] * jnp.dot(
            left, right, preferred_element_type=F32
        )
        total = term if total is None else total + term
    return total


def body(green_function, couplings, phonon_modes, weights):
    tile, slab = green_function.shape[1:]
    group = slab // tile
    levels = group.bit_length() - 1
    stops, modes = phonon_modes.shape
    width = 2 * tile

    def kernel(name, function, args, outs, specs=None, scratch=(), limit=12, flops=0):
        return pl.pallas_call(
            function,
            in_specs=specs or [VMEM] * len(args),
            out_specs=[VMEM] * len(outs),
            out_shape=[jax.ShapeDtypeStruct(*out) for out in outs],
            scratch_shapes=list(scratch),
            compiler_params=pltpu.CompilerParams(vmem_limit_bytes=limit << 20),
            cost_estimate=pl.CostEstimate(flops=flops, transcendentals=0, bytes_accessed=4096),
            name=name,
        )(*args)

    incoming = passed_along(green_function, "mom", group)
    prepared = kernel(
        "prepare",
        prepare_kernel,
        [phonon_modes, couplings],
        [((modes, 2, slab, slab), BF16), ((modes, slab, width), BF16)] * stops,
        specs=[HBM, HBM],
        scratch=[
            pltpu.SMEM((stops, modes), jnp.int32),
            pltpu.SemaphoreType.DMA,
            pltpu.SemaphoreType.DMA((stops, modes)),
        ],
        limit=38,
    )
    picked, turned = prepared[::2], prepared[1::2]
    own_blocks = gathered(green_function, "mom", levels, turned[0])

    def later(*refs):
        *blocks, weights, turned, picked, leaving, spectral = refs
        fill_spectral(blocks, spectral)
        leaving[...] = stop_term(0, weights, spectral, turned, picked, None).astype(BF16)

    leaving, spectral = kernel(
        "later_stop",
        later,
        [*own_blocks, weights, turned[0], picked[0]],
        [((slab, width), BF16), ((slab, 2 * slab), BF16)],
        flops=2147483648,
    )
    arrived = passed_along(leaving, "mom", -group)

    def own(spectral, weights, turned, picked, out):
        out[...] = stop_term(1, weights, spectral, turned, picked, None)

    (total,) = kernel(
        "own_stop", own, [spectral, weights, turned[1], picked[1]], [((slab, width), F32)], flops=2147483648
    )

    def earlier(*refs):
        *blocks, weights, turned, picked, before, out, spectral = refs
        fill_spectral(blocks, spectral)
        out[...] = stop_term(2, weights, spectral, turned, picked, before[...])

    next_blocks = gathered(incoming, "mom", levels, leaving)
    (total,) = kernel(
        "earlier_stop",
        earlier,
        [*next_blocks, weights, turned[2], picked[2], total],
        [((slab, width), F32)],
        scratch=[pltpu.VMEM((slab, 2 * slab), BF16)],
        flops=2147483648,
    )

    def finish(total, arrived, out):
        whole = total[...] + arrived[...].astype(F32)
        out[0] = whole[:, :tile].T
        out[1] = -whole[:, tile:].T

    (rows,) = kernel("finish", finish, [total, arrived], [((2, tile, slab), F32)])
    return rows


def solution(mesh):
    in_specs = (P(None, ("grp", "mom"), None), P(), P(), P())
    out_specs = P(None, ("grp", "mom"), None)
    return jax.shard_map(body, mesh=mesh, in_specs=in_specs, out_specs=out_specs, check_vma=False)
```

```python
import jax
import jax.numpy as jnp
from jax import lax
from jax.experimental import pallas as pl
from jax.experimental.pallas import tpu as pltpu
from jax.sharding import PartitionSpec as P

F32 = jnp.float32
BF16 = jnp.bfloat16
VMEM = pl.BlockSpec(memory_space=pltpu.VMEM)
ANY = pl.BlockSpec(memory_space=pl.ANY)


def partner(block, axis, bit):
    count = lax.axis_size(axis)
    return lax.ppermute(block, axis, [(i, i ^ 1 << bit) for i in range(count)])


def passed_along(block, axis, distance):
    count = lax.axis_size(axis)
    return lax.ppermute(block, axis, [((i - distance) % count, i) for i in range(count)])


def after(value, *before):
    return lax.optimization_barrier((value, *before))[0]


def gathered(block, axis, levels, before, halves=None):
    have = {0: block}
    for level in reversed(range(levels)):
        for offset in list(have):
            moving = have[offset] if offset == 0 else after(have[offset], before)
            if halves and offset:
                have[offset | 1 << level] = tuple(partner(part, axis, level) for part in halves(moving))
            else:
                have[offset | 1 << level] = partner(moving, axis, level)
    return [have[offset] for offset in sorted(have)]


def beside(first, second):
    return jnp.concatenate([first, second], axis=1)


def own_row(offset, group, tile):
    member = lax.axis_index("mom") % group
    return pl.multiple_of((member ^ offset) * tile, tile)


def fill_spectral(blocks, spectral):
    tile, slab = blocks[0].shape[1:]
    reals = [block[0] if isinstance(block, tuple) else block.at[0] for block in blocks]
    imags = [block[1] if isinstance(block, tuple) else block.at[1] for block in blocks]
    starts = [own_row(offset, len(blocks), tile) for offset in range(len(blocks))]
    spots = [pl.ds(start, tile) for start in starts]
    imag_spots = [pl.ds(slab + start, tile) for start in starts]
    for i in range(len(blocks)):
        for j in range(len(blocks)):
            real = -(imags[i][:, spots[j]].astype(F32) + imags[j][:, spots[i]].T.astype(F32))
            imag = reals[i][:, spots[j]].astype(F32) - reals[j][:, spots[i]].T.astype(F32)
            spectral[spots[i], spots[j]] = real.astype(BF16)
            spectral[spots[i], imag_spots[j]] = imag.astype(BF16)


def stop_term(stop, weights, spectral, turned, couplings, chosen, listing, start):
    count, slab, width = turned.shape
    tile = width // 2
    rights = []
    for mode in range(count):
        real, imag = turned[mode, :, :tile], turned[mode, :, tile:]
        rights.append(jnp.concatenate([beside(real, -imag), beside(imag, real)], axis=0))
    products = jnp.dot(
        spectral[...], jnp.concatenate(rights, axis=1), preferred_element_type=F32
    ).astype(BF16)
    listing.wait()
    total = start
    for mode in range(count):
        product = products[:, mode * width : (mode + 1) * width]
        real, imag = product[:, :tile], product[:, tile:]
        right = jnp.concatenate([product, beside(-imag, real)], axis=0)
        index = chosen[stop, mode]
        left = beside(couplings[index, 0], couplings[index, 1])
        term = weights[stop : stop + 1, mode : mode + 1] * jnp.dot(
            left, right, preferred_element_type=F32
        )
        total = term if total is None else total + term
    return total


def body(green_function, couplings, phonon_modes, weights):
    tile, slab = green_function.shape[1:]
    group = slab // tile
    levels = group.bit_length() - 1
    stops, modes = phonon_modes.shape
    width = 2 * tile
    term_shape = (slab, width)
    spectral_shape = (slab, 2 * slab)

    def kernel(name, function, args, outs, scratch=()):
        def started(listed, *refs):
            *refs, chosen, sem = refs
            listing = pltpu.make_async_copy(listed, chosen, sem)
            listing.start()
            function(listing, chosen, *refs)

        return pl.pallas_call(
            started,
            in_specs=[ANY] + [VMEM] * (len(args) - 1),
            out_specs=[VMEM] * len(outs),
            out_shape=[jax.ShapeDtypeStruct(*out) for out in outs],
            scratch_shapes=[*scratch, pltpu.SMEM((stops, modes), jnp.int32), pltpu.SemaphoreType.DMA],
            compiler_params=pltpu.CompilerParams(vmem_limit_bytes=12 << 20),
            cost_estimate=pl.CostEstimate(flops=0, transcendentals=0, bytes_accessed=4096),
            name=name,
        )(*args)

    def prepare(listing, chosen, couplings, *turned):
        listing.wait()
        rows = pl.ds(own_row(0, group, tile), tile)
        for stop in range(stops):
            for mode in range(modes):
                index = chosen[stop, mode]
                turned[stop][mode, :, :tile] = couplings[index, 0, rows, :].T
                turned[stop][mode, :, tile:] = couplings[index, 1, rows, :].T

    incoming = passed_along(green_function, "mom", group)
    turned = kernel("prepare", prepare, [phonon_modes, couplings], [((modes, slab, width), BF16)] * stops)
    own_blocks = gathered(green_function, "mom", levels, turned[0])

    def later(listing, chosen, *refs):
        *blocks, weights, turned, couplings, leaving, spectral = refs
        fill_spectral(blocks, spectral)
        leaving[...] = stop_term(
            0, weights, spectral, turned, couplings, chosen, listing, None
        ).astype(BF16)

    leaving, spectral = kernel(
        "later_stop",
        later,
        [phonon_modes, *own_blocks, weights, turned[0], couplings],
        [(term_shape, BF16), (spectral_shape, BF16)],
    )
    arrived = passed_along(leaving, "mom", -group)

    def own(listing, chosen, spectral, weights, turned, couplings, out):
        out[...] = stop_term(1, weights, spectral, turned, couplings, chosen, listing, None)

    (total,) = kernel(
        "own_stop", own, [phonon_modes, spectral, weights, turned[1], couplings], [(term_shape, F32)]
    )

    def halves(block):
        def split(block, real, imag):
            real[...] = block[0]
            imag[...] = block[1]

        half = jax.ShapeDtypeStruct(block.shape[1:], block.dtype)
        return pl.pallas_call(
            split,
            in_specs=[VMEM],
            out_specs=[VMEM] * 2,
            out_shape=[half] * 2,
            compiler_params=pltpu.CompilerParams(vmem_limit_bytes=4 << 20),
            cost_estimate=pl.CostEstimate(flops=0, transcendentals=0, bytes_accessed=4096),
            name="split",
        )(block)

    next_blocks = gathered(incoming, "mom", levels, total, halves)

    def earlier(listing, chosen, *refs):
        *parts, weights, turned, couplings, before, out, spectral = refs
        parts = iter(parts)
        blocks = [(next(parts), next(parts)) if isinstance(b, tuple) else next(parts) for b in next_blocks]
        fill_spectral(blocks, spectral)
        out[...] = stop_term(2, weights, spectral, turned, couplings, chosen, listing, before[...])

    (total,) = kernel(
        "earlier_stop",
        earlier,
        [phonon_modes, *jax.tree.leaves(next_blocks), weights, turned[2], couplings, total],
        [(term_shape, F32)],
        [pltpu.VMEM(spectral_shape, BF16)],
    )

    def finish(total, arrived, out):
        whole = total[...] + arrived[...].astype(F32)
        out[0] = whole[:, :tile].T
        out[1] = -whole[:, tile:].T

    return pl.pallas_call(
        finish,
        in_specs=[VMEM, VMEM],
        out_specs=VMEM,
        out_shape=jax.ShapeDtypeStruct((2, tile, slab), F32),
        compiler_params=pltpu.CompilerParams(vmem_limit_bytes=4 << 20),
        cost_estimate=pl.CostEstimate(flops=0, transcendentals=0, bytes_accessed=4096),
        name="finish",
    )(total, arrived)


def solution(mesh):
    in_specs = (P(None, ("grp", "mom"), None), P(), P(), P())
    out_specs = P(None, ("grp", "mom"), None)
    return jax.shard_map(body, mesh=mesh, in_specs=in_specs, out_specs=out_specs, check_vma=False)
```

```python
import jax
import jax.numpy as jnp
from jax import lax
from jax.experimental import pallas as pl
from jax.experimental.pallas import tpu as pltpu
from jax.sharding import PartitionSpec as P

F32 = jnp.float32
BF16 = jnp.bfloat16
VMEM = pl.BlockSpec(memory_space=pltpu.VMEM)
ANY = pl.BlockSpec(memory_space=pl.ANY)


def moved(block, axis, route):
    return lax.ppermute(block, axis, [(i, route(i)) for i in range(lax.axis_size(axis))])


def passed_along(block, axis, distance):
    count = lax.axis_size(axis)
    return moved(block, axis, lambda i: (i + distance) % count)


def partner(block, axis, bit):
    return moved(block, axis, lambda i: i ^ 1 << bit)


def after(value, *before):
    return lax.optimization_barrier((value, *before))[0]


def spread(have, top):
    for level in reversed(range(top)):
        for offset, block in list(have.items()):
            if isinstance(block, tuple):
                have[offset | 1 << level] = tuple(partner(part, "mom", level) for part in block[1:])
            else:
                have[offset | 1 << level] = partner(block, "mom", level)
    return [
        block[0] if isinstance(block, tuple) and len(block) == 3 else block
        for _, block in sorted(have.items())
    ]


def beside(first, second):
    return jnp.concatenate([first, second], axis=1)


def own_row(offset, group, tile):
    member = lax.axis_index("mom") % group
    return pl.multiple_of((member ^ offset) * tile, tile)


def fill_spectral(blocks, spectral):
    tile, slab = blocks[0].shape[1:]
    reals = [block[0] if isinstance(block, tuple) else block.at[0] for block in blocks]
    imags = [block[1] if isinstance(block, tuple) else block.at[1] for block in blocks]
    starts = [own_row(offset, len(blocks), tile) for offset in range(len(blocks))]
    spots = [pl.ds(start, tile) for start in starts]
    imag_spots = [pl.ds(slab + start, tile) for start in starts]
    for i in range(len(blocks)):
        for j in range(len(blocks)):
            real = -(imags[i][:, spots[j]].astype(F32) + imags[j][:, spots[i]].T.astype(F32))
            imag = reals[i][:, spots[j]].astype(F32) - reals[j][:, spots[i]].T.astype(F32)
            spectral[spots[i], spots[j]] = real.astype(BF16)
            spectral[spots[i], imag_spots[j]] = imag.astype(BF16)


def stop_term(stop, weights, spectral, turned, couplings, chosen, listing, start):
    count, slab, width = turned.shape
    tile = width // 2
    rights = []
    for mode in range(count):
        real, imag = turned[mode, :, :tile], turned[mode, :, tile:]
        rights.append(jnp.concatenate([beside(real, -imag), beside(imag, real)], axis=0))
    products = jnp.dot(
        spectral[...], jnp.concatenate(rights, axis=1), preferred_element_type=F32
    ).astype(BF16)
    listing.wait()
    total = start
    for mode in range(count):
        product = products[:, mode * width : (mode + 1) * width]
        real, imag = product[:, :tile], product[:, tile:]
        right = jnp.concatenate([product, beside(-imag, real)], axis=0)
        index = chosen[stop, mode]
        left = beside(couplings[index, 0], couplings[index, 1])
        term = weights[stop : stop + 1, mode : mode + 1] * jnp.dot(
            left, right, preferred_element_type=F32
        )
        total = term if total is None else total + term
    return total


def body(green_function, couplings, phonon_modes, weights):
    tile, slab = green_function.shape[1:]
    group = slab // tile
    levels = group.bit_length() - 1
    stops, modes = phonon_modes.shape
    width = 2 * tile
    term_shape = (slab, width)
    spectral_shape = (slab, 2 * slab)

    def kernel(name, function, args, outs, scratch=()):
        def started(listed, *refs):
            *refs, chosen, sem = refs
            listing = pltpu.make_async_copy(listed, chosen, sem)
            listing.start()
            function(listing, chosen, *refs)

        return pl.pallas_call(
            started,
            in_specs=[ANY] + [VMEM] * (len(args) - 1),
            out_specs=[VMEM] * len(outs),
            out_shape=[jax.ShapeDtypeStruct(*out) for out in outs],
            scratch_shapes=[*scratch, pltpu.SMEM((stops, modes), jnp.int32), pltpu.SemaphoreType.DMA],
            compiler_params=pltpu.CompilerParams(vmem_limit_bytes=12 << 20),
            cost_estimate=pl.CostEstimate(flops=0, transcendentals=0, bytes_accessed=4096),
            name=name,
        )(*args)

    def prepare(listing, chosen, couplings, *turned):
        listing.wait()
        rows = pl.ds(own_row(0, group, tile), tile)
        for stop in range(stops):
            for mode in range(modes):
                index = chosen[stop, mode]
                turned[stop][mode, :, :tile] = couplings[index, 0, rows, :].T
                turned[stop][mode, :, tile:] = couplings[index, 1, rows, :].T

    def quick(name, function, args, outs):
        return pl.pallas_call(
            function,
            in_specs=[VMEM] * len(args),
            out_specs=[VMEM] * len(outs),
            out_shape=[jax.ShapeDtypeStruct(*out) for out in outs],
            compiler_params=pltpu.CompilerParams(vmem_limit_bytes=4 << 20),
            cost_estimate=pl.CostEstimate(flops=0, transcendentals=0, bytes_accessed=4096),
            name=name,
        )(*args)

    def choose(even, odd, out):
        member = lax.axis_index("mom") % 2

        @pl.when(member == 0)
        def _():
            out[...] = even[...]

        @pl.when(member == 1)
        def _():
            out[...] = odd[...]

    top = levels - 1
    incoming = passed_along(green_function, "mom", group)
    turned = kernel("prepare", prepare, [phonon_modes, couplings], [((modes, slab, width), BF16)] * stops)
    far = partner(green_function, "mom", top)
    ready = after(far, turned[0], incoming)
    own_blocks = spread({0: green_function, 1 << top: ready}, top)
    (leaves,) = quick("choose", choose, [incoming, ready], [(green_function.shape, BF16)])
    count = lax.axis_size("mom")
    next_far = moved(leaves, "mom", lambda i: (i + group) % count if i % 2 else i ^ 1 << top)

    def later(listing, chosen, *refs):
        *blocks, weights, turned, couplings, leaving, spectral = refs
        fill_spectral(blocks, spectral)
        leaving[...] = stop_term(
            0, weights, spectral, turned, couplings, chosen, listing, None
        ).astype(BF16)

    leaving, spectral = kernel(
        "later_stop",
        later,
        [phonon_modes, *own_blocks, weights, turned[0], couplings],
        [(term_shape, BF16), (spectral_shape, BF16)],
    )
    arrived = passed_along(leaving, "mom", -group)

    def own(listing, chosen, spectral, weights, turned, couplings, out):
        out[...] = stop_term(1, weights, spectral, turned, couplings, chosen, listing, None)

    (total,) = kernel(
        "own_stop", own, [phonon_modes, spectral, weights, turned[1], couplings], [(term_shape, F32)]
    )

    def split(block, real, imag):
        real[...] = block[0]
        imag[...] = block[1]

    real, imag = quick("split", split, [after(next_far, leaving)], [((tile, slab), BF16)] * 2)
    next_blocks = spread({0: incoming, 1 << top: (next_far, real, imag)}, top)

    def earlier(listing, chosen, *refs):
        *parts, weights, turned, couplings, before, out, spectral = refs
        parts = iter(parts)
        blocks = [(next(parts), next(parts)) if isinstance(b, tuple) else next(parts) for b in next_blocks]
        fill_spectral(blocks, spectral)
        out[...] = stop_term(2, weights, spectral, turned, couplings, chosen, listing, before[...])

    (total,) = kernel(
        "earlier_stop",
        earlier,
        [phonon_modes, *jax.tree.leaves(next_blocks), weights, turned[2], couplings, total],
        [(term_shape, F32)],
        [pltpu.VMEM(spectral_shape, BF16)],
    )

    def finish(total, arrived, out):
        whole = total[...] + arrived[...].astype(F32)
        out[0] = whole[:, :tile].T
        out[1] = -whole[:, tile:].T

    (rows,) = quick("finish", finish, [total, arrived], [((2, tile, slab), F32)])
    return rows


def solution(mesh):
    in_specs = (P(None, ("grp", "mom"), None), P(), P(), P())
    out_specs = P(None, ("grp", "mom"), None)
    return jax.shard_map(body, mesh=mesh, in_specs=in_specs, out_specs=out_specs, check_vma=False)
```

```python
import jax
import jax.numpy as jnp
from jax import lax
from jax.experimental import pallas as pl
from jax.experimental.pallas import tpu as pltpu
from jax.sharding import PartitionSpec as P

F32 = jnp.float32
BF16 = jnp.bfloat16
VMEM = pl.BlockSpec(memory_space=pltpu.VMEM)
ANY = pl.BlockSpec(memory_space=pl.ANY)


def moved(block, axis, route):
    return lax.ppermute(block, axis, [(i, route(i)) for i in range(lax.axis_size(axis))])


def passed_along(block, axis, distance):
    count = lax.axis_size(axis)
    return moved(block, axis, lambda i: (i + distance) % count)


def partner(block, axis, bit):
    return moved(block, axis, lambda i: i ^ 1 << bit)


def after(value, *before):
    return lax.optimization_barrier((value, *before))[0]


def spread(have, top):
    for level in reversed(range(top)):
        for offset, block in list(have.items()):
            if isinstance(block, tuple):
                have[offset | 1 << level] = tuple(partner(part, "mom", level) for part in block[1:])
            else:
                have[offset | 1 << level] = partner(block, "mom", level)
    return [
        block[0] if isinstance(block, tuple) and len(block) == 3 else block
        for _, block in sorted(have.items())
    ]


def beside(first, second):
    return jnp.concatenate([first, second], axis=1)


def own_row(offset, group, tile):
    member = lax.axis_index("mom") % group
    return pl.multiple_of((member ^ offset) * tile, tile)


def fill_spectral(blocks, spectral):
    tile, slab = blocks[0].shape[1:]
    reals = [block[0] if isinstance(block, tuple) else block.at[0] for block in blocks]
    imags = [block[1] if isinstance(block, tuple) else block.at[1] for block in blocks]
    starts = [own_row(offset, len(blocks), tile) for offset in range(len(blocks))]
    spots = [pl.ds(start, tile) for start in starts]
    imag_spots = [pl.ds(slab + start, tile) for start in starts]
    for i in range(len(blocks)):
        for j in range(len(blocks)):
            real = -(imags[i][:, spots[j]].astype(F32) + imags[j][:, spots[i]].T.astype(F32))
            imag = reals[i][:, spots[j]].astype(F32) - reals[j][:, spots[i]].T.astype(F32)
            spectral[spots[i], spots[j]] = real.astype(BF16)
            spectral[spots[i], imag_spots[j]] = imag.astype(BF16)


def triangle(tile):
    row = lax.broadcasted_iota(jnp.int32, (tile, tile), 0)
    column = lax.broadcasted_iota(jnp.int32, (tile, tile), 1)
    return row <= column


def packed(total, group, leaving, whole):
    tile = total.shape[1] // 2
    whole[...] = total
    for offset in range(1, group):
        spot = slice((offset - 1) * tile, offset * tile)
        leaving[spot] = whole[pl.ds(own_row(offset, group, tile), tile), :].astype(BF16)
    own = whole[pl.ds(own_row(0, group, tile), tile), :]
    both = jnp.where(triangle(tile), own[:, :tile], own[:, tile:])
    half = tile // 2
    leaving[(group - 1) * tile :] = beside(both[:half], both[half:]).astype(BF16)


def add_packed(whole, arrived, group):
    tile = whole.shape[1] // 2
    for offset in range(1, group):
        spot = pl.ds(own_row(offset, group, tile), tile)
        whole[spot, :] += arrived[(offset - 1) * tile : offset * tile].astype(F32)
    both = arrived[(group - 1) * tile :].astype(F32)
    both = jnp.concatenate([both[:, :tile], both[:, tile:]], axis=0)
    turned = both.T
    upper = triangle(tile)
    row = lax.broadcasted_iota(jnp.int32, (tile, tile), 0)
    column = lax.broadcasted_iota(jnp.int32, (tile, tile), 1)
    real = jnp.where(upper, both, turned)
    imag = jnp.where(row > column, both, jnp.where(row < column, -turned, 0.0))
    whole[pl.ds(own_row(0, group, tile), tile), :] += beside(real, imag)


def stop_term(stop, weights, spectral, turned, couplings, chosen, listing, start):
    count, slab, width = turned.shape
    tile = width // 2
    rights = []
    for mode in range(count):
        real, imag = turned[mode, :, :tile], turned[mode, :, tile:]
        rights.append(jnp.concatenate([beside(real, -imag), beside(imag, real)], axis=0))
    products = jnp.dot(
        spectral[...], jnp.concatenate(rights, axis=1), preferred_element_type=F32
    ).astype(BF16)
    listing.wait()
    total = start
    for mode in range(count):
        product = products[:, mode * width : (mode + 1) * width]
        real, imag = product[:, :tile], product[:, tile:]
        right = jnp.concatenate([product, beside(-imag, real)], axis=0)
        index = chosen[stop, mode]
        left = beside(couplings[index, 0], couplings[index, 1])
        term = weights[stop : stop + 1, mode : mode + 1] * jnp.dot(
            left, right, preferred_element_type=F32
        )
        total = term if total is None else total + term
    return total


def body(green_function, couplings, phonon_modes, weights):
    tile, slab = green_function.shape[1:]
    group = slab // tile
    levels = group.bit_length() - 1
    stops, modes = phonon_modes.shape
    width = 2 * tile
    term_shape = (slab, width)
    spectral_shape = (slab, 2 * slab)

    def kernel(name, function, args, outs, scratch=()):
        def started(listed, *refs):
            *refs, chosen, sem = refs
            listing = pltpu.make_async_copy(listed, chosen, sem)
            listing.start()
            function(listing, chosen, *refs)

        return pl.pallas_call(
            started,
            in_specs=[ANY] + [VMEM] * (len(args) - 1),
            out_specs=[VMEM] * len(outs),
            out_shape=[jax.ShapeDtypeStruct(*out) for out in outs],
            scratch_shapes=[*scratch, pltpu.SMEM((stops, modes), jnp.int32), pltpu.SemaphoreType.DMA],
            compiler_params=pltpu.CompilerParams(vmem_limit_bytes=12 << 20),
            cost_estimate=pl.CostEstimate(flops=0, transcendentals=0, bytes_accessed=4096),
            name=name,
        )(*args)

    def prepare(listing, chosen, couplings, *turned):
        listing.wait()
        rows = pl.ds(own_row(0, group, tile), tile)
        for stop in range(stops):
            for mode in range(modes):
                index = chosen[stop, mode]
                turned[stop][mode, :, :tile] = couplings[index, 0, rows, :].T
                turned[stop][mode, :, tile:] = couplings[index, 1, rows, :].T

    def quick(name, function, args, outs):
        return pl.pallas_call(
            function,
            in_specs=[VMEM] * len(args),
            out_specs=[VMEM] * len(outs),
            out_shape=[jax.ShapeDtypeStruct(*out) for out in outs],
            compiler_params=pltpu.CompilerParams(vmem_limit_bytes=4 << 20),
            cost_estimate=pl.CostEstimate(flops=0, transcendentals=0, bytes_accessed=4096),
            name=name,
        )(*args)

    def choose(even, odd, out):
        member = lax.axis_index("mom") % 2

        @pl.when(member == 0)
        def _():
            out[...] = even[...]

        @pl.when(member == 1)
        def _():
            out[...] = odd[...]

    top = levels - 1
    incoming = passed_along(green_function, "mom", group)
    turned = kernel("prepare", prepare, [phonon_modes, couplings], [((modes, slab, width), BF16)] * stops)
    far = partner(green_function, "mom", top)
    ready = after(far, turned[0], incoming)
    own_blocks = spread({0: green_function, 1 << top: ready}, top)
    (leaves,) = quick("choose", choose, [incoming, ready], [(green_function.shape, BF16)])
    count = lax.axis_size("mom")
    next_far = moved(leaves, "mom", lambda i: (i + group) % count if i % 2 else i ^ 1 << top)

    def later(listing, chosen, *refs):
        *blocks, weights, turned, couplings, leaving, spectral, whole = refs
        fill_spectral(blocks, spectral)
        total = stop_term(0, weights, spectral, turned, couplings, chosen, listing, None)
        packed(total, group, leaving, whole)

    leaving, spectral = kernel(
        "later_stop",
        later,
        [phonon_modes, *own_blocks, weights, turned[0], couplings],
        [((slab - tile // 2, width), BF16), (spectral_shape, BF16)],
        [pltpu.VMEM(term_shape, F32)],
    )
    arrived = passed_along(leaving, "mom", -group)

    def own(listing, chosen, spectral, weights, turned, couplings, out):
        out[...] = stop_term(1, weights, spectral, turned, couplings, chosen, listing, None)

    (total,) = kernel(
        "own_stop", own, [phonon_modes, spectral, weights, turned[1], couplings], [(term_shape, F32)]
    )

    def split(block, real, imag):
        real[...] = block[0]
        imag[...] = block[1]

    real, imag = quick("split", split, [after(next_far, leaving)], [((tile, slab), BF16)] * 2)
    next_blocks = spread({0: incoming, 1 << top: (next_far, real, imag)}, top)

    def earlier(listing, chosen, *refs):
        *parts, weights, turned, couplings, before, out, spectral = refs
        parts = iter(parts)
        blocks = [(next(parts), next(parts)) if isinstance(b, tuple) else next(parts) for b in next_blocks]
        fill_spectral(blocks, spectral)
        out[...] = stop_term(2, weights, spectral, turned, couplings, chosen, listing, before[...])

    (total,) = kernel(
        "earlier_stop",
        earlier,
        [phonon_modes, *jax.tree.leaves(next_blocks), weights, turned[2], couplings, total],
        [(term_shape, F32)],
        [pltpu.VMEM(spectral_shape, BF16)],
    )

    def finish(total, arrived, out, whole, rows, sems):
        whole[...] = total[...]
        add_packed(whole, arrived, group)
        copies = [pltpu.make_async_copy(rows.at[half], out.at[half], sems.at[half]) for half in range(2)]
        rows[0] = whole[:, :tile].T
        copies[0].start()
        rows[1] = -whole[:, tile:].T
        copies[1].start()
        for copy in copies:
            copy.wait()

    return pl.pallas_call(
        finish,
        in_specs=[VMEM] * 2,
        out_specs=ANY,
        out_shape=jax.ShapeDtypeStruct((2, tile, slab), F32),
        scratch_shapes=[
            pltpu.VMEM(term_shape, F32),
            pltpu.VMEM((2, tile, slab), F32),
            pltpu.SemaphoreType.DMA((2,)),
        ],
        compiler_params=pltpu.CompilerParams(vmem_limit_bytes=6 << 20),
        cost_estimate=pl.CostEstimate(flops=0, transcendentals=0, bytes_accessed=4096),
        name="finish",
    )(total, arrived)


def solution(mesh):
    in_specs = (P(None, ("grp", "mom"), None), P(), P(), P())
    out_specs = P(None, ("grp", "mom"), None)
    return jax.shard_map(body, mesh=mesh, in_specs=in_specs, out_specs=out_specs, check_vma=False)
```

```python
import jax
import jax.numpy as jnp
from jax import lax
from jax.experimental import pallas as pl
from jax.experimental.pallas import tpu as pltpu
from jax.sharding import PartitionSpec as P

F32 = jnp.float32
BF16 = jnp.bfloat16
VMEM = pl.BlockSpec(memory_space=pltpu.VMEM)
ANY = pl.BlockSpec(memory_space=pl.ANY)


def moved(block, axis, route):
    return lax.ppermute(block, axis, [(i, route(i)) for i in range(lax.axis_size(axis))])


def passed_along(block, axis, distance):
    count = lax.axis_size(axis)
    return moved(block, axis, lambda i: (i + distance) % count)


def partner(block, axis, bit):
    return moved(block, axis, lambda i: i ^ 1 << bit)


def after(value, *before):
    return lax.optimization_barrier((value, *before))[0]


def spread(have, top):
    for level in reversed(range(top)):
        for offset, block in list(have.items()):
            if isinstance(block, tuple):
                have[offset | 1 << level] = tuple(partner(part, "mom", level) for part in block[1:])
            else:
                have[offset | 1 << level] = partner(block, "mom", level)
    return [
        block[0] if isinstance(block, tuple) and len(block) == 3 else block
        for _, block in sorted(have.items())
    ]


def beside(first, second):
    return jnp.concatenate([first, second], axis=1)


def own_row(offset, group, tile):
    member = lax.axis_index("mom") % group
    return pl.multiple_of((member ^ offset) * tile, tile)


def fill_spectral(blocks, spectral):
    tile, slab = blocks[0].shape[1:]
    reals = [block[0] if isinstance(block, tuple) else block.at[0] for block in blocks]
    imags = [block[1] if isinstance(block, tuple) else block.at[1] for block in blocks]
    starts = [own_row(offset, len(blocks), tile) for offset in range(len(blocks))]
    spots = [pl.ds(start, tile) for start in starts]
    imag_spots = [pl.ds(slab + start, tile) for start in starts]
    for i in range(len(blocks)):
        for j in range(len(blocks)):
            real = -(imags[i][:, spots[j]].astype(F32) + imags[j][:, spots[i]].T.astype(F32))
            imag = reals[i][:, spots[j]].astype(F32) - reals[j][:, spots[i]].T.astype(F32)
            spectral[spots[i], spots[j]] = real.astype(BF16)
            spectral[spots[i], imag_spots[j]] = imag.astype(BF16)


def triangle(tile):
    row = lax.broadcasted_iota(jnp.int32, (tile, tile), 0)
    column = lax.broadcasted_iota(jnp.int32, (tile, tile), 1)
    return row <= column


def packed(total, group, leaving, whole):
    tile = total.shape[1] // 2
    whole[...] = total
    for offset in range(1, group):
        spot = slice((offset - 1) * tile, offset * tile)
        leaving[spot] = whole[pl.ds(own_row(offset, group, tile), tile), :].astype(BF16)
    own = whole[pl.ds(own_row(0, group, tile), tile), :]
    both = jnp.where(triangle(tile), own[:, :tile], own[:, tile:])
    half = tile // 2
    leaving[(group - 1) * tile :] = beside(both[:half], both[half:]).astype(BF16)


def add_packed(whole, arrived, group):
    tile = whole.shape[1] // 2
    for offset in range(1, group):
        spot = pl.ds(own_row(offset, group, tile), tile)
        whole[spot, :] += arrived[(offset - 1) * tile : offset * tile].astype(F32)
    both = arrived[(group - 1) * tile :].astype(F32)
    both = jnp.concatenate([both[:, :tile], both[:, tile:]], axis=0)
    turned = both.T
    upper = triangle(tile)
    row = lax.broadcasted_iota(jnp.int32, (tile, tile), 0)
    column = lax.broadcasted_iota(jnp.int32, (tile, tile), 1)
    real = jnp.where(upper, both, turned)
    imag = jnp.where(row > column, both, jnp.where(row < column, -turned, 0.0))
    whole[pl.ds(own_row(0, group, tile), tile), :] += beside(real, imag)


def stop_term(stop, weights, spectral, turned, picked, start, modes=None):
    count, slab, width = turned.shape
    tile = width // 2
    rights = []
    modes = range(count) if modes is None else modes
    for mode in modes:
        real, imag = turned[mode, :, :tile], turned[mode, :, tile:]
        rights.append(jnp.concatenate([beside(real, -imag), beside(imag, real)], axis=0))
    products = jnp.dot(
        spectral[...], jnp.concatenate(rights, axis=1), preferred_element_type=F32
    ).astype(BF16)
    total = start
    for place, mode in enumerate(modes):
        product = products[:, place * width : (place + 1) * width]
        real, imag = product[:, :tile], product[:, tile:]
        right = jnp.concatenate([product, beside(-imag, real)], axis=0)
        left = beside(picked[mode, 0], picked[mode, 1])
        term = weights[stop : stop + 1, mode : mode + 1] * jnp.dot(
            left, right, preferred_element_type=F32
        )
        total = term if total is None else total + term
    return total


def body(green_function, couplings, phonon_modes, weights):
    tile, slab = green_function.shape[1:]
    group = slab // tile
    levels = group.bit_length() - 1
    stops, modes = phonon_modes.shape
    width = 2 * tile
    term_shape = (slab, width)
    spectral_shape = (slab, 2 * slab)

    def kernel(name, function, args, outs, scratch=(), leading=VMEM):
        return pl.pallas_call(
            function,
            in_specs=[leading] + [VMEM] * (len(args) - 1),
            out_specs=[VMEM] * len(outs),
            out_shape=[jax.ShapeDtypeStruct(*out) for out in outs],
            scratch_shapes=list(scratch),
            compiler_params=pltpu.CompilerParams(vmem_limit_bytes=12 << 20),
            cost_estimate=pl.CostEstimate(flops=0, transcendentals=0, bytes_accessed=4096),
            name=name,
        )(*args)

    def prepare(listed, couplings, *refs):
        picked, turned = refs[:stops], refs[stops : 2 * stops]
        chosen, listed_sem, sems = refs[2 * stops :]
        listing = pltpu.make_async_copy(listed, chosen, listed_sem)
        listing.start()
        listing.wait()
        copies = [
            pltpu.make_async_copy(couplings.at[chosen[stop, mode]], picked[stop].at[mode], sems.at[stop, mode])
            for stop in range(stops)
            for mode in range(modes)
        ]
        for copy in copies:
            copy.start()
        rows = pl.ds(own_row(0, group, tile), tile)
        for stop in range(stops):
            for mode in range(modes):
                index = chosen[stop, mode]
                turned[stop][mode, :, :tile] = couplings[index, 0, rows, :].T
                turned[stop][mode, :, tile:] = couplings[index, 1, rows, :].T
        for copy in copies:
            copy.wait()

    def quick(name, function, args, outs):
        return pl.pallas_call(
            function,
            in_specs=[VMEM] * len(args),
            out_specs=[VMEM] * len(outs),
            out_shape=[jax.ShapeDtypeStruct(*out) for out in outs],
            compiler_params=pltpu.CompilerParams(vmem_limit_bytes=4 << 20),
            cost_estimate=pl.CostEstimate(flops=0, transcendentals=0, bytes_accessed=4096),
            name=name,
        )(*args)

    def choose(even, odd, out):
        member = lax.axis_index("mom") % 2

        @pl.when(member == 0)
        def _():
            out[...] = even[...]

        @pl.when(member == 1)
        def _():
            out[...] = odd[...]

    top = levels - 1
    incoming = passed_along(green_function, "mom", group)
    prepared = kernel(
        "prepare",
        prepare,
        [phonon_modes, couplings],
        [((modes, 2, slab, slab), BF16)] * stops + [((modes, slab, width), BF16)] * stops,
        [
            pltpu.SMEM((stops, modes), jnp.int32),
            pltpu.SemaphoreType.DMA,
            pltpu.SemaphoreType.DMA((stops, modes)),
        ],
        ANY,
    )
    picked, turned = prepared[:stops], prepared[stops:]
    far = partner(green_function, "mom", top)
    ready = after(far, turned[0])
    own_blocks = spread({0: green_function, 1 << top: ready}, top)
    (leaves,) = quick("choose", choose, [incoming, ready], [(green_function.shape, BF16)])
    count = lax.axis_size("mom")
    next_far = moved(leaves, "mom", lambda i: (i + group) % count if i % 2 else i ^ 1 << top)

    def later(*refs):
        *blocks, weights, turned, picked, leaving, spectral, whole = refs
        fill_spectral(blocks, spectral)
        total = stop_term(0, weights, spectral, turned, picked, None)
        packed(total, group, leaving, whole)

    leaving, spectral = kernel(
        "later_stop",
        later,
        [*own_blocks, weights, turned[0], picked[0]],
        [((slab - tile // 2, width), BF16), (spectral_shape, BF16)],
        [pltpu.VMEM(term_shape, F32)],
    )
    arrived = passed_along(leaving, "mom", -group)

    def own(spectral, weights, turned, picked, out):
        out[...] = stop_term(1, weights, spectral, turned, picked, None, range(modes // 2))

    def own_rest(spectral, weights, turned, picked, before, out):
        rest = range(modes // 2, modes)
        out[...] = stop_term(1, weights, spectral, turned, picked, before[...], rest)

    own_args = [spectral, weights, turned[1], picked[1]]
    (begun,) = kernel("own_stop", own, own_args, [(term_shape, F32)])

    def split(block, real, imag):
        real[...] = block[0]
        imag[...] = block[1]

    real, imag = quick("split", split, [after(next_far, begun)], [((tile, slab), BF16)] * 2)
    own_args[0] = after(spectral, real)
    (total,) = kernel("own_rest", own_rest, [*own_args, begun], [(term_shape, F32)])
    next_blocks = spread({0: incoming, 1 << top: (next_far, real, imag)}, top)

    def earlier(*refs):
        *parts, weights, turned, picked, before, out, spectral = refs
        parts = iter(parts)
        blocks = [(next(parts), next(parts)) if isinstance(b, tuple) else next(parts) for b in next_blocks]
        fill_spectral(blocks, spectral)
        out[...] = stop_term(2, weights, spectral, turned, picked, before[...])

    (total,) = kernel(
        "earlier_stop",
        earlier,
        [*jax.tree.leaves(next_blocks), weights, turned[2], picked[2], total],
        [(term_shape, F32)],
        [pltpu.VMEM(spectral_shape, BF16)],
    )

    def finish(total, arrived, out, whole, rows, sems):
        whole[...] = total[...]
        add_packed(whole, arrived, group)
        copies = [pltpu.make_async_copy(rows.at[half], out.at[half], sems.at[half]) for half in range(2)]
        rows[0] = whole[:, :tile].T
        copies[0].start()
        rows[1] = -whole[:, tile:].T
        copies[1].start()
        for copy in copies:
            copy.wait()

    return pl.pallas_call(
        finish,
        in_specs=[VMEM] * 2,
        out_specs=ANY,
        out_shape=jax.ShapeDtypeStruct((2, tile, slab), F32),
        scratch_shapes=[
            pltpu.VMEM(term_shape, F32),
            pltpu.VMEM((2, tile, slab), F32),
            pltpu.SemaphoreType.DMA((2,)),
        ],
        compiler_params=pltpu.CompilerParams(vmem_limit_bytes=6 << 20),
        cost_estimate=pl.CostEstimate(flops=0, transcendentals=0, bytes_accessed=4096),
        name="finish",
    )(total, arrived)


def solution(mesh):
    in_specs = (P(None, ("grp", "mom"), None), P(), P(), P())
    out_specs = P(None, ("grp", "mom"), None)
    return jax.shard_map(body, mesh=mesh, in_specs=in_specs, out_specs=out_specs, check_vma=False)
```

```python
import jax
import jax.numpy as jnp
from jax import lax
from jax.experimental import pallas as pl
from jax.experimental.pallas import tpu as pltpu
from jax.sharding import PartitionSpec as P

F32 = jnp.float32
BF16 = jnp.bfloat16
VMEM = pl.BlockSpec(memory_space=pltpu.VMEM)
ANY = pl.BlockSpec(memory_space=pl.ANY)


def moved(block, axis, route):
    return lax.ppermute(block, axis, [(i, route(i)) for i in range(lax.axis_size(axis))])


def passed_along(block, axis, distance):
    count = lax.axis_size(axis)
    return moved(block, axis, lambda i: (i + distance) % count)


def partner(block, axis, bit):
    return moved(block, axis, lambda i: i ^ 1 << bit)


def after(value, *before):
    return lax.optimization_barrier((value, *before))[0]


def spread(have, top):
    for level in reversed(range(top)):
        for offset, block in list(have.items()):
            if isinstance(block, tuple):
                have[offset | 1 << level] = tuple(partner(part, "mom", level) for part in block[1:])
            else:
                have[offset | 1 << level] = partner(block, "mom", level)
    return [
        block[0] if isinstance(block, tuple) and len(block) == 3 else block
        for _, block in sorted(have.items())
    ]


def beside(first, second):
    return jnp.concatenate([first, second], axis=1)


def own_row(offset, group, tile):
    member = lax.axis_index("mom") % group
    return pl.multiple_of((member ^ offset) * tile, tile)


def fill_spectral(blocks, spectral):
    tile, slab = blocks[0].shape[1:]
    reals = [block[0] if isinstance(block, tuple) else block.at[0] for block in blocks]
    imags = [block[1] if isinstance(block, tuple) else block.at[1] for block in blocks]
    starts = [own_row(offset, len(blocks), tile) for offset in range(len(blocks))]
    spots = [pl.ds(start, tile) for start in starts]
    imag_spots = [pl.ds(slab + start, tile) for start in starts]
    for i in range(len(blocks)):
        for j in range(len(blocks)):
            real = -(imags[i][:, spots[j]].astype(F32) + imags[j][:, spots[i]].T.astype(F32))
            imag = reals[i][:, spots[j]].astype(F32) - reals[j][:, spots[i]].T.astype(F32)
            spectral[spots[i], spots[j]] = real.astype(BF16)
            spectral[spots[i], imag_spots[j]] = imag.astype(BF16)


def triangle(tile):
    row = lax.broadcasted_iota(jnp.int32, (tile, tile), 0)
    column = lax.broadcasted_iota(jnp.int32, (tile, tile), 1)
    return row <= column


def packed(total, group, leaving, whole):
    tile = total.shape[1] // 2
    whole[...] = total.astype(BF16)
    for offset in range(1, group):
        spot = slice((offset - 1) * tile, offset * tile)
        leaving[spot] = whole[pl.ds(own_row(offset, group, tile), tile), :]
    own = whole[pl.ds(own_row(0, group, tile), tile), :]
    both = jnp.where(triangle(tile), own[:, :tile], own[:, tile:])
    half = tile // 2
    leaving[(group - 1) * tile :] = beside(both[:half], both[half:])


def packed_part(arrived, group, part):
    tile = arrived.shape[1] // 2
    columns = slice(part * tile, (part + 1) * tile)
    for offset in range(1, group):
        turned = arrived[(offset - 1) * tile : offset * tile, columns].T.astype(F32)
        yield offset, -turned if part else turned
    both = arrived[(group - 1) * tile :].astype(F32)
    both = jnp.concatenate([both[:, :tile], both[:, tile:]], axis=0)
    turned = both.T
    row = lax.broadcasted_iota(jnp.int32, (tile, tile), 0)
    column = lax.broadcasted_iota(jnp.int32, (tile, tile), 1)
    if part:
        yield 0, jnp.where(row > column, both, jnp.where(row < column, -turned, 0.0))
    else:
        yield 0, jnp.where(row <= column, both, turned)


def stop_term(stop, weights, spectral, turned, picked, start, modes=None):
    count, slab, width = turned.shape
    tile = width // 2
    rights = []
    modes = range(count) if modes is None else modes
    for mode in modes:
        real, imag = turned[mode, :, :tile], turned[mode, :, tile:]
        rights.append(jnp.concatenate([beside(real, -imag), beside(imag, real)], axis=0))
    products = jnp.dot(
        spectral[...], jnp.concatenate(rights, axis=1), preferred_element_type=F32
    ).astype(BF16)
    total = start
    for place, mode in enumerate(modes):
        product = products[:, place * width : (place + 1) * width]
        real, imag = product[:, :tile], product[:, tile:]
        right = jnp.concatenate([product, beside(-imag, real)], axis=0)
        left = beside(picked[mode, 0], picked[mode, 1])
        term = weights[stop : stop + 1, mode : mode + 1] * jnp.dot(
            left, right, preferred_element_type=F32
        )
        total = term if total is None else total + term
    return total


def body(green_function, couplings, phonon_modes, weights):
    tile, slab = green_function.shape[1:]
    group = slab // tile
    levels = group.bit_length() - 1
    stops, modes = phonon_modes.shape
    width = 2 * tile
    term_shape = (slab, width)
    spectral_shape = (slab, 2 * slab)

    def kernel(name, function, args, outs, scratch=(), leading=VMEM):
        return pl.pallas_call(
            function,
            in_specs=[leading] + [VMEM] * (len(args) - 1),
            out_specs=[VMEM] * len(outs),
            out_shape=[jax.ShapeDtypeStruct(*out) for out in outs],
            scratch_shapes=list(scratch),
            compiler_params=pltpu.CompilerParams(vmem_limit_bytes=12 << 20),
            cost_estimate=pl.CostEstimate(flops=0, transcendentals=0, bytes_accessed=4096),
            name=name,
        )(*args)

    def prepare(listed, couplings, *refs):
        picked, turned = refs[:stops], refs[stops : 2 * stops]
        chosen, listed_sem, sems = refs[2 * stops :]
        listing = pltpu.make_async_copy(listed, chosen, listed_sem)
        listing.start()
        listing.wait()
        copies = [
            pltpu.make_async_copy(couplings.at[chosen[stop, mode]], picked[stop].at[mode], sems.at[stop, mode])
            for stop in range(stops)
            for mode in range(modes)
        ]
        for copy in copies:
            copy.start()
        rows = pl.ds(own_row(0, group, tile), tile)
        for stop in range(stops):
            for mode in range(modes):
                index = chosen[stop, mode]
                turned[stop][mode, :, :tile] = couplings[index, 0, rows, :].T
                turned[stop][mode, :, tile:] = couplings[index, 1, rows, :].T
        for copy in copies:
            copy.wait()

    def quick(name, function, args, outs):
        return pl.pallas_call(
            function,
            in_specs=[VMEM] * len(args),
            out_specs=[VMEM] * len(outs),
            out_shape=[jax.ShapeDtypeStruct(*out) for out in outs],
            compiler_params=pltpu.CompilerParams(vmem_limit_bytes=4 << 20),
            cost_estimate=pl.CostEstimate(flops=0, transcendentals=0, bytes_accessed=4096),
            name=name,
        )(*args)

    def choose(even, odd, out):
        member = lax.axis_index("mom") % 2

        @pl.when(member == 0)
        def _():
            out[...] = even[...]

        @pl.when(member == 1)
        def _():
            out[...] = odd[...]

    top = levels - 1
    incoming = passed_along(green_function, "mom", group)
    prepared = kernel(
        "prepare",
        prepare,
        [phonon_modes, couplings],
        [((modes, 2, slab, slab), BF16)] * stops + [((modes, slab, width), BF16)] * stops,
        [
            pltpu.SMEM((stops, modes), jnp.int32),
            pltpu.SemaphoreType.DMA,
            pltpu.SemaphoreType.DMA((stops, modes)),
        ],
        ANY,
    )
    picked, turned = prepared[:stops], prepared[stops:]
    far = partner(green_function, "mom", top)
    ready = after(far, turned[0])
    own_blocks = spread({0: green_function, 1 << top: ready}, top)
    (leaves,) = quick("choose", choose, [incoming, ready], [(green_function.shape, BF16)])
    count = lax.axis_size("mom")
    next_far = moved(leaves, "mom", lambda i: (i + group) % count if i % 2 else i ^ 1 << top)

    def later(*refs):
        *blocks, weights, turned, picked, leaving, spectral, whole = refs
        fill_spectral(blocks, spectral)
        total = stop_term(0, weights, spectral, turned, picked, None)
        packed(total, group, leaving, whole)

    leaving, spectral = kernel(
        "later_stop",
        later,
        [*own_blocks, weights, turned[0], picked[0]],
        [((slab - tile // 2, width), BF16), (spectral_shape, BF16)],
        [pltpu.VMEM(term_shape, BF16)],
    )
    arrived = passed_along(leaving, "mom", -group)

    def own(spectral, weights, turned, picked, out):
        out[...] = stop_term(1, weights, spectral, turned, picked, None, range(modes // 2))

    def own_rest(spectral, weights, turned, picked, before, out):
        rest = range(modes // 2, modes)
        out[...] = stop_term(1, weights, spectral, turned, picked, before[...], rest)

    own_args = [spectral, weights, turned[1], picked[1]]
    (begun,) = kernel("own_stop", own, own_args, [(term_shape, F32)])

    def split(block, real, imag):
        real[...] = block[0]
        imag[...] = block[1]

    real, imag = quick("split", split, [after(next_far, begun)], [((tile, slab), BF16)] * 2)
    own_args[0] = after(spectral, real)
    (total,) = kernel("own_rest", own_rest, [*own_args, begun], [(term_shape, F32)])
    next_blocks = spread({0: incoming, 1 << top: (next_far, real, imag)}, top)

    def earlier(*refs):
        *parts, weights, turned, picked, before, out, spectral = refs
        parts = iter(parts)
        blocks = [(next(parts), next(parts)) if isinstance(b, tuple) else next(parts) for b in next_blocks]
        fill_spectral(blocks, spectral)
        total = stop_term(2, weights, spectral, turned, picked, before[...])
        out[0] = total[:, :tile].T
        out[1] = -total[:, tile:].T

    (total,) = kernel(
        "earlier_stop",
        earlier,
        [*jax.tree.leaves(next_blocks), weights, turned[2], picked[2], total],
        [((2, tile, slab), F32)],
        [pltpu.VMEM(spectral_shape, BF16)],
    )

    def finish(total, arrived, out, rows, sems):
        copies = []
        for part in range(2):
            for offset, block in packed_part(arrived, group, part):
                spot = pl.ds(own_row(offset, group, tile), tile)
                rows[part, :, spot] = total[part, :, spot] + block
            copies.append(pltpu.make_async_copy(rows.at[part], out.at[part], sems.at[part]))
            copies[part].start()
        for copy in copies:
            copy.wait()

    return pl.pallas_call(
        finish,
        in_specs=[VMEM] * 2,
        out_specs=ANY,
        out_shape=jax.ShapeDtypeStruct((2, tile, slab), F32),
        scratch_shapes=[
            pltpu.VMEM((2, tile, slab), F32),
            pltpu.SemaphoreType.DMA((2,)),
        ],
        compiler_params=pltpu.CompilerParams(vmem_limit_bytes=6 << 20),
        cost_estimate=pl.CostEstimate(flops=0, transcendentals=0, bytes_accessed=4096),
        name="finish",
    )(total, arrived)


def solution(mesh):
    in_specs = (P(None, ("grp", "mom"), None), P(), P(), P())
    out_specs = P(None, ("grp", "mom"), None)
    return jax.shard_map(body, mesh=mesh, in_specs=in_specs, out_specs=out_specs, check_vma=False)
```
